32 devices in a mesh: space: 8 (over z, y), slab: 4 (over x, core).
Axes of the slice: x: 2, y: 2, z: 4, core: 2. Of those that a mesh axis runs over, the one named last changes fastest.
Arguments:
- features: float32 [128, 8, 8, 512], P(('space', 'slab')), may hold values from -6 to 6
- live: int32 [32], P(('space', 'slab')), may hold values from 1 to 4, as said below
- rim_slots: int32 [32, 2], P(('space', 'slab')), may hold values from 0 to 3, as said below
- neighbours: int32 [128, 26], P(('space', 'slab')), may hold values from 0 to 12, as said below
- weights: float32 [4, 27, 4096], replicated, may hold values from -0.15625 to 0.15625
- biases: float32 [4, 64], replicated, may hold values from -3 to 3
Outputs:
- output: float32 [128, 8, 8, 512], P(('space', 'slab'))
The draws below stay inside these ranges and needn't reach their ends.
Inputs may be any that keep to these rules, and one draw needn't show every extreme that they name: `live`: devices whose space indices differ by 8 / 2 (same slab index) hold at most 6 occupied bricks together; in every draw some pair holds exactly that and some device holds 4. `rim_slots`: every entry is below its device's live count. `neighbours`: entries below 4 are below the device's live count.
All inputs are finite; a program needn't handle non-finite values.
Results may differ from the reference program's by a relative error of at most 0.0003.
Values sent between devices are 32-bit elements; how exact they have to be, the bound alone decides.
A program may use at most 128 MiB of HBM per device.

```python
import jax
import jax.numpy as jnp
from jax import lax

CH = 64
CONVS = 4
B_DEV = 4
RIM = 2
LEND = 3
BRICKS = 128
N_SPACE = 8
N_SLAB = 4


def live_counts(key):
    base = jax.random.fold_in(key, 11)
    kone, ktwo, kthree, kfour = jax.random.split(base, 4)
    half = N_SPACE // 2
    pairs = half * N_SLAB
    heavy = jax.random.randint(kone, (pairs,), LEND, B_DEV + 1)
    spread = jax.random.randint(ktwo, (pairs,), 0, 1 << 20)
    light = 1 + spread % (2 * LEND - heavy)
    forced = jax.random.randint(kthree, (), 0, pairs)
    index = jnp.arange(pairs)
    heavy = jnp.where(index == forced, B_DEV, heavy)
    light = jnp.where(index == forced, 2 * LEND - B_DEV, light)
    flip = jax.random.randint(kfour, (pairs,), 0, 2)
    first = jnp.where(flip == 1, heavy, light).reshape(half, N_SLAB)
    second = jnp.where(flip == 1, light, heavy).reshape(half, N_SLAB)
    return jnp.concatenate([first, second], 0).reshape(-1).astype(jnp.int32)


def draw_live(key, part):
    return live_counts(key)


def draw_rim_slots(key, part):
    counts = live_counts(key)
    spread = jax.random.randint(jax.random.fold_in(key, 23), (N_SPACE * N_SLAB, RIM), 0, 1 << 20)
    return (spread % counts[:, None]).astype(jnp.int32)


def draw_neighbours(key, part):
    counts = live_counts(key)
    rows = N_SPACE * N_SLAB * B_DEV
    owner_live = jnp.repeat(counts, B_DEV)[:, None]
    kone, ktwo = jax.random.split(jax.random.fold_in(key, 37))
    kind = jax.random.randint(kone, (rows, 26), 0, 5)
    spread = jax.random.randint(ktwo, (rows, 26), 0, 1 << 20)
    own = spread % owner_live
    rim = B_DEV + spread % (4 * RIM)
    empty = jnp.full((rows, 26), B_DEV + 4 * RIM, jnp.int32)
    return jnp.where(kind < 2, own, jnp.where(kind < 4, rim, empty)).astype(jnp.int32)


def block_scale(stream_key, dims, cuts, smallest, top_value):
    level = 1.0
    for axis_at, blocks in cuts:
        heights = jax.random.uniform(jax.random.fold_in(jax.random.fold_in(stream_key, 6), axis_at), (blocks,), jnp.float32, smallest / len(cuts), top_value / len(cuts))
        level = level * jnp.repeat(jnp.exp(heights), dims[axis_at] // blocks).reshape((-1,) + (1,) * (len(dims) - 1 - axis_at))
    return level


def noise(stream_key, shape, deviation, most, cuts=(), held_as=jnp.bfloat16):
    factor_of = block_scale(stream_key, shape, cuts, -0.22, 0.18) if cuts else 1.0
    array = jax.random.normal(stream_key, shape, jnp.float32) * deviation * factor_of
    return jnp.minimum(jnp.maximum(array, -most), most).astype(held_as)


def setup_inputs(seed: int = 0) -> dict:
    arg_keys = jax.random.split(jax.random.key(seed), 7)
    return {
        "features": noise(arg_keys[0], (BRICKS, 8, 8, 8 * CH), 1.0, 6.0, ((0, 32),), jnp.float32),
        "live": draw_live(jax.random.fold_in(arg_keys[6], 71), 0),
        "rim_slots": draw_rim_slots(jax.random.fold_in(arg_keys[6], 71), 0),
        "neighbours": draw_neighbours(jax.random.fold_in(arg_keys[6], 71), 0),
        "weights": noise(arg_keys[4], (CONVS, 27, CH * CH), (27 * CH) ** -0.5, 0.15625, (), jnp.float32),
        "biases": noise(arg_keys[5], (CONVS, CH), 0.5, 3.0, (), jnp.float32),
    }


def direction_list():
    result = []
    for ddx in (-1, 0, 1):
        for ddy in (-1, 0, 1):
            for ddz in (-1, 0, 1):
                if (ddx, ddy, ddz) != (0, 0, 0):
                    result.append((ddx, ddy, ddz))
    return result


def source_index(step):
    if step == -1:
        return 7
    if step == 1:
        return 0
    return slice(0, 8)


def extent(step):
    return 8 if step == 0 else 1


def brick_piece(table, direction):
    ddx, ddy, ddz = direction
    channels = table.shape[-1] // 8
    cube = table.reshape(table.shape[0], 8, 8, 8, channels)
    return cube[:, source_index(ddx), source_index(ddy), source_index(ddz)]


def assemble(center, table, nbr, getter):
    count = center.shape[0]
    channels = center.shape[-1] // 8
    blocks = {(0, 0, 0): center.reshape(count, 8, 8, 8, channels)}
    for jdir, direction in enumerate(direction_list()):
        piece = getter(table, direction)[nbr[:, jdir]]
        blocks[direction] = piece.reshape(count, extent(direction[0]), extent(direction[1]), extent(direction[2]), channels)
    slabs = []
    for ddx in (-1, 0, 1):
        rows = []
        for ddy in (-1, 0, 1):
            rows.append(jnp.concatenate([blocks[(ddx, ddy, ddz)] for ddz in (-1, 0, 1)], 3))
        slabs.append(jnp.concatenate(rows, 2))
    return jnp.concatenate(slabs, 1)


def convolve(padded, kernel):
    count = padded.shape[0]
    channels = padded.shape[-1]
    taps = kernel.reshape(27, channels, channels)
    stacked = jnp.concatenate([padded[:, :, boff:boff + 8, coff:coff + 8, :] for boff in range(3) for coff in range(3)], -1)
    total = jnp.zeros((count * 512, channels), jnp.float32)
    for aoff in range(3):
        columns = stacked[:, aoff:aoff + 8].reshape(count * 512, 9 * channels)
        block = taps[aoff * 9:aoff * 9 + 9].reshape(9 * channels, channels)
        total = total + jnp.dot(columns, block, preferred_element_type=jnp.float32, precision=lax.Precision.HIGHEST)
    return total.reshape(count, 8, 8, 8 * channels)


def reference(features, live, rim_slots, neighbours, weights, biases):
    devices = N_SPACE * N_SLAB
    width = 8 * CH
    field = features.reshape(devices, B_DEV, 8, 8, width)
    mask = (jnp.arange(B_DEV, dtype=jnp.int32)[None, :] < live[:, None]).astype(jnp.float32)[:, :, None, None, None]
    nbr = neighbours.reshape(devices, B_DEV, 26)

    def layer(field, kidx):
        rims = jax.vmap(lambda rows, slots: rows[slots])(field, rim_slots)
        grid = rims.reshape(N_SPACE, N_SLAB, RIM, 8, 8, width)
        zero_row = jnp.zeros((1, N_SLAB, RIM, 8, 8, width), jnp.float32)
        zero_col = jnp.zeros((N_SPACE, 1, RIM, 8, 8, width), jnp.float32)
        low_space = jnp.concatenate([zero_row, grid[:-1]], 0)
        high_space = jnp.concatenate([grid[1:], zero_row], 0)
        low_slab = jnp.concatenate([zero_col, grid[:, :-1]], 1)
        high_slab = jnp.concatenate([grid[:, 1:], zero_col], 1)
        beside_all = jnp.concatenate([low_space, high_space, low_slab, high_slab], 2).reshape(devices, 4 * RIM, 8, 8, width)
        table = jnp.concatenate([field, beside_all, jnp.zeros((devices, 1, 8, 8, width), jnp.float32)], 1)

        def single(items):
            tab, cen, nb = items
            return convolve(assemble(cen, tab, nb, brick_piece), weights[kidx])

        return lax.map(single, (table, field, nbr))

    field = field * mask
    for blk in range(CONVS // 2):
        first = 2 * blk
        hidden = jax.nn.relu(layer(field, first) + jnp.tile(biases[first], 8)) * mask
        field = jax.nn.relu(field + layer(hidden, first + 1) + jnp.tile(biases[first + 1], 8)) * mask
    return field.reshape(devices * B_DEV, 8, 8, width)
```

```python
import functools

import jax
import jax.numpy as jnp
from jax import lax
from jax.experimental import pallas as pl
from jax.experimental.pallas import tpu as pltpu
from jax.sharding import PartitionSpec as P

MESH = pl.DeviceIdType.MESH
SIDE = 8
RELAYED = 4


def direction_number(dx, dy, dz):
    index = 9 * (dx + 1) + 3 * (dy + 1) + (dz + 1)
    return index if index < 13 else index - 1


def layers_kernel(
    nsp, nsl, nbr, live, rim, feat, bias, w_hbm, out,
    cur, hid, offx, offy, offz, pad, cols, whi, wlo, wbuf, blk, acc,
    emap, inv, perm, nb, wsem, ssem, rsem, *tabs,
):
    bricks = feat.shape[0]
    width = feat.shape[-1]
    ch = width // SIDE
    half = width // 2
    pair = 2 * ch
    ktile = half + pair
    kdy = 3 * ktile
    rims = offx.shape[1]
    convs = w_hbm.shape[2]
    tabx, taby, tabz = tabs[:convs], tabs[convs:2 * convs], tabs[2 * convs:]
    last = bricks + 4 * rims
    sp = lax.axis_index("space")
    sl = lax.axis_index("slab")
    odd = lax.rem(sp, 2)

    near = (sp + 1 - 2 * odd, sl)
    far = (sp - 1 + 2 * odd, sl)
    via = (sp - 2 + 4 * odd, sl)
    onto = (sp + 2 - 4 * odd, sl)
    has_far = jnp.where(odd == 1, sp < nsp - 1, sp > 0)
    has_onto = jnp.where(odd == 1, sp > 1, sp < nsp - 2)
    lower = (sl > 0, (sp, sl - 1))
    upper = (sl < nsl - 1, (sp, sl + 1))
    near_first = bricks + rims * (1 - odd)
    far_first = bricks + rims * odd

    barrier = pltpu.get_barrier_semaphore()
    greeted = ((sp >= 0, near), (has_far, far), (has_far, via), (has_onto, onto), lower, upper)
    for has, peer in greeted:
        @pl.when(has)
        def _():
            pl.semaphore_signal(barrier, inc=1, device_id=peer, device_id_type=MESH)

    def weight_copy(k):
        return pltpu.make_async_copy(w_hbm.at[:, :, k], wbuf.at[k], wsem.at[k])

    for k in range(convs):
        weight_copy(k).start()

    chunks = [(j, part) for j in range(rims) for part in range(3)]
    relayed = min(RELAYED, len(chunks))

    def offered(k, j, part):
        if part == 0:
            return offx.at[k, j]
        if part == 1:
            return offy.at[k, j, :, 1:SIDE - 1, :]
        return offz.at[k, j]

    def entry_of(k, at, part):
        if part == 0:
            return tabx[k].at[at]
        if part == 1:
            return taby[k].at[at, :, 1:SIDE - 1, :]
        return tabz[k].at[at]

    def copy(k, src, dst, flow, index, peer):
        return pltpu.make_async_remote_copy(
            src_ref=src, dst_ref=dst, send_sem=ssem.at[k, flow, index],
            recv_sem=rsem.at[k, flow, index], device_id=peer, device_id_type=MESH,
        )

    def to_near(k, c):
        j, part = chunks[c]
        return copy(k, offered(k, j, part), entry_of(k, far_first + j, part), 0, c, near)

    def from_near(k, c):
        j, part = chunks[c]
        return copy(k, offered(k, j, part), entry_of(k, near_first + j, part), 0, c, near)

    def to_far(k, c):
        j, part = chunks[c]
        return copy(k, offered(k, j, part), entry_of(k, near_first + j, part), 1, c, far)

    def relay(k, c):
        j, part = chunks[c]
        return copy(
            k, entry_of(k, near_first + j, part), entry_of(k, far_first + j, part), 1, c, onto
        )

    def from_far(k, c):
        j, part = chunks[c]
        return copy(k, offered(k, j, part), entry_of(k, far_first + j, part), 1, c, far)

    def beside(k, d, j, part, to):
        first = bricks + rims * (d ^ 1 if to else d)
        index = 3 * j + part
        peer = (lower if d == 2 else upper)[1]
        return pltpu.make_async_remote_copy(
            src_ref=offered(k, j, part), dst_ref=entry_of(k, first + j, part),
            send_sem=ssem.at[k, d, index], recv_sem=rsem.at[k, d ^ 1 if to else d, index],
            device_id=peer, device_id_type=MESH,
        )

    def send(k):
        for c in range(relayed):
            to_near(k, c).start()
        for c in range(relayed, len(chunks)):
            to_near(k, c).start()

            @pl.when(has_far)
            def _():
                to_far(k, c).start()
        for d, (has, _) in ((2, lower), (3, upper)):
            @pl.when(has)
            def _():
                for j, part in chunks:
                    beside(k, d, j, part, True).start()

    def pass_on(k, some):
        for c in some:
            from_near(k, c).wait_recv()

            @pl.when(has_onto)
            def _():
                relay(k, c).start()

    def receive(k):
        for c in range(relayed, len(chunks)):
            from_near(k, c).wait_recv()
        for d, (has, _) in ((2, lower), (3, upper)):
            @pl.when(has)
            def _():
                for j, part in chunks:
                    beside(k, d, j, part, False).wait_recv()

        @pl.when(has_far)
        def _():
            for c in range(len(chunks)):
                from_far(k, c).wait_recv()

    def finish_sends(k):
        for c in range(len(chunks)):
            to_near(k, c).wait_send()

        @pl.when(has_far)
        def _():
            for c in range(relayed, len(chunks)):
                to_far(k, c).wait_send()

        @pl.when(has_onto)
        def _():
            for c in range(relayed):
                relay(k, c).wait_send()
        for d, (has, _) in ((2, lower), (3, upper)):
            @pl.when(has)
            def _():
                for j, part in chunks:
                    beside(k, d, j, part, True).wait_send()

    slots = [rim[0, j] for j in range(rims)]
    score = []
    for b in range(bricks):
        s = rims + b
        for j in reversed(range(rims)):
            s = jnp.where(slots[j] == b, j, s)
        score.append(s)
    place = [
        sum(jnp.where(score[o] < score[b], 1, 0) for o in range(bricks) if o != b)
        for b in range(bricks)
    ]
    held = [
        sum(jnp.where(place[b] == p, b, 0) for b in range(bricks)) for p in range(bricks)
    ]
    for b in range(bricks):
        inv[b] = place[b]
        perm[b] = held[b]
    spot = [sum(jnp.where(slots[j] == b, place[b], 0) for b in range(bricks)) for j in range(rims)]

    def mask_of(b):
        return jnp.where(b < live[0], 1.0, 0.0).astype(jnp.float32)

    low = lax.broadcasted_iota(jnp.int32, (SIDE, pair), 1) < ch
    low1 = lax.broadcasted_iota(jnp.int32, (1, pair), 1) < ch
    loww = lax.broadcasted_iota(jnp.int32, wbuf.shape[2:], 1) < ch

    def take_faces(src, k, group):
        def one(p, carry):
            tabx[k][p, 0] = src[p, 0]
            tabx[k][p, 1] = src[p, SIDE - 1]
            for s, y in ((0, 0), (1, SIDE - 1)):
                for x in range(1, SIDE - 1):
                    taby[k][p, s, x:x + 1, :] = src[p, x, y:y + 1, :]
            for x in range(1, SIDE - 1):
                at = (x - 1) * pair
                tabz[k][p, :, at:at + pair] = jnp.where(
                    low, src[p, x, :, 0:pair], src[p, x, :, width - pair:width]
                )
            return carry

        lax.fori_loop(group[0], group[1], one, 0)

    def make_offer(k):
        for j in range(rims):
            for off, tab in ((offx, tabx[k]), (offy, taby[k]), (offz, tabz[k])):
                value = tab[0]
                for p in range(1, j + 1):
                    value = jnp.where(spot[j] == p, tab[p], value)
                off[k, j] = value

    def build_weights(k):
        weight_copy(k).wait()

        def one(t, carry):
            a = t // 3
            base = pl.multiple_of((t - 3 * a) * ktile, ktile)
            taps = [wbuf[k, 3 * t + i] for i in range(3)]
            turned = [pltpu.roll(tap, ch, 1) for tap in taps]
            none = jnp.zeros(taps[0].shape, jnp.float32)
            rows = taps[0].shape[0]
            for j in range(4):
                first, first_turned = (taps[j], turned[j]) if j < 3 else (none, none)
                second, second_turned = (taps[j - 1], turned[j - 1]) if j > 0 else (none, none)
                blk[j, pl.ds(0, rows, stride=2), :] = jnp.where(loww, first, second_turned)
                blk[j, pl.ds(1, rows, stride=2), :] = jnp.where(loww, first_turned, second)
            for j in range(4):
                block = blk[j]
                hi = block.astype(jnp.bfloat16)
                lo = (block - hi.astype(jnp.float32)).astype(jnp.bfloat16)
                for q in range(2):
                    z = j - 1 + 2 * q
                    row = base + (z if z >= 0 else 5) * ch
                    row = pl.multiple_of(row, ch)
                    lanes = slice(q * pair, (q + 1) * pair)
                    whi[a, pl.ds(row, ch), lanes] = hi
                    whi[a, pl.ds(pl.multiple_of(row + kdy, ch), ch), lanes] = hi
                    wlo[a, pl.ds(row, ch), lanes] = lo
            return carry

        lax.fori_loop(0, 9, one, 0)

    def row_of(center, below, above, mask):
        return jnp.concatenate(
            [
                center[:, :half],
                jnp.where(mask, center[:, half:half + pair], below),
                center[:, half:],
                jnp.where(mask, above, center[:, half - pair:half]),
            ],
            axis=1,
        )

    def build_columns(src, k, group, at_of):
        tx, ty, tz = tabx[k], taby[k], tabz[k]

        def one(i, carry):
            p = at_of(group[0] + i)

            def entry(dx, dy, dz):
                return nb[p, direction_number(dx, dy, dz)]

            def x_row(dx, dy, s, y):
                return row_of(
                    tx[entry(dx, dy, 0), s, y:y + 1, :],
                    tx[entry(dx, dy, -1), s, y:y + 1, width - pair:width],
                    tx[entry(dx, dy, 1), s, y:y + 1, 0:pair],
                    low1,
                )

            for dx, xrow, s in ((-1, 0, 1), (1, SIDE + 1, 0)):
                pad[xrow, 1:SIDE + 1, :] = row_of(
                    tx[entry(dx, 0, 0), s],
                    tx[entry(dx, 0, -1), s, :, width - pair:width],
                    tx[entry(dx, 0, 1), s, :, 0:pair],
                    low,
                )
                for dy, yrow, y in ((-1, 0, SIDE - 1), (1, SIDE + 1, 0)):
                    pad[xrow, yrow:yrow + 1, :] = x_row(dx, dy, s, y)
            nlow, nhigh = entry(0, 0, -1), entry(0, 0, 1)
            for x in range(SIDE):
                if x in (0, SIDE - 1):
                    s = 0 if x == 0 else 1
                    below = tx[nlow, s, :, width - pair:width]
                    above = tx[nhigh, s, :, 0:pair]
                else:
                    at = (x - 1) * pair
                    below = tz[nlow, :, at:at + pair]
                    above = tz[nhigh, :, at:at + pair]
                pad[1 + x, 1:SIDE + 1, :] = row_of(src[p, x], below, above, low)
            for dy, yrow, s, y in ((-1, 0, 1, SIDE - 1), (1, SIDE + 1, 0, 0)):
                rows = row_of(
                    ty[entry(0, dy, 0), s],
                    ty[entry(0, dy, -1), s, :, width - pair:width],
                    ty[entry(0, dy, 1), s, :, 0:pair],
                    low,
                )
                for x in range(1, SIDE - 1):
                    pad[1 + x, yrow:yrow + 1, :] = rows[x:x + 1]
                pad[1, yrow:yrow + 1, :] = x_row(0, dy, 0, y)
                pad[SIDE, yrow:yrow + 1, :] = x_row(0, dy, 1, y)
            at = pl.multiple_of(i * 2 * SIDE, 2 * SIDE)
            for x in range(SIDE + 2):
                for dy in range(3):
                    v = pad[x, dy:dy + SIDE, :]
                    v = jnp.concatenate([v[:, :ktile], v[:, ktile:]], axis=0)
                    hi = v.astype(jnp.bfloat16)
                    lo = (v - hi.astype(jnp.float32)).astype(jnp.bfloat16)
                    cols[x, pl.ds(at, 2 * SIDE), dy * ktile:(dy + 1) * ktile] = hi
                    cols[x, pl.ds(at, 2 * SIDE), kdy + dy * ktile:kdy + (dy + 1) * ktile] = lo
            return carry

        lax.fori_loop(0, group[1] - group[0], one, 0)

    def convolve(group):
        tall = (group[1] - group[0]) * 2 * SIDE
        steps = SIDE // 2
        totals = [None, None]
        for a in range(3):
            for h in range(2):
                x = a + h * steps
                left = cols[x:x + steps, :tall].reshape(steps * tall, 2 * kdy)
                term = jnp.dot(left, whi[a], preferred_element_type=jnp.float32)
                totals[h] = term if totals[h] is None else totals[h] + term
                left = cols[x:x + steps, :tall, :kdy].reshape(steps * tall, kdy)
                totals[h] = totals[h] + jnp.dot(left, wlo[a], preferred_element_type=jnp.float32)
        for h in range(2):
            acc[h * steps:(h + 1) * steps, :tall] = totals[h].reshape(steps, tall, half)

    def epilogue(k, res, dst, group, at_of):
        bvec = bias[k:k + 1, :]
        bvec = jnp.concatenate([bvec, bvec, bvec, bvec], axis=1)

        def one(i, carry):
            b = group[0] + i
            p = at_of(b)
            m = mask_of(perm[p])
            for x in range(SIDE):
                for t in range(2):
                    at = pl.multiple_of(i * 2 * SIDE + t * SIDE, SIDE)
                    v = acc[x, pl.ds(at, SIDE), :] + bvec
                    lanes = slice(t * half, (t + 1) * half)
                    if res is not None:
                        v = v + res[p, x, :, lanes]
                    dst[b, x, :, lanes] = jnp.maximum(v, 0.0) * m
            return carry

        lax.fori_loop(0, group[1] - group[0], one, 0)

    def mask_features(p, carry):
        cur[p] = feat[perm[p]] * mask_of(perm[p])
        return carry

    first = (0, rims)
    rest = (rims, bricks)
    lax.fori_loop(0, bricks, mask_features, 0)
    take_faces(cur, 0, first)
    make_offer(0)
    arrivals = sum(jnp.where(has, 1, 0) for has, _ in greeted)
    pl.semaphore_wait(barrier, arrivals)
    send(0)

    take_faces(cur, 0, rest)
    for k in range(convs):
        for tab in (tabx[k], taby[k], tabz[k]):
            tab[last] = jnp.zeros(tab.shape[1:], jnp.float32)
    for e in range(last + 1):
        if e < bricks:
            emap[e] = place[e]
        elif e < bricks + rims:
            emap[e] = jnp.where(sp > 0, e, last)
        elif e < bricks + 2 * rims:
            emap[e] = jnp.where(sp < nsp - 1, e, last)
        elif e < bricks + 3 * rims:
            emap[e] = jnp.where(sl > 0, e, last)
        elif e < last:
            emap[e] = jnp.where(sl < nsl - 1, e, last)
        else:
            emap[e] = last

    def remap(j, carry):
        for p in range(bricks):
            nb[p, j] = emap[nbr[perm[p], j]]
        return carry

    lax.fori_loop(0, nbr.shape[1], remap, 0)
    whi[...] = jnp.zeros_like(whi)
    wlo[...] = jnp.zeros_like(wlo)
    build_weights(0)
    pass_on(0, range(relayed))

    for k in range(convs):
        src = cur if k % 2 == 0 else hid
        res = None if k % 2 == 0 else cur
        receive(k)
        if k < convs - 1:
            dst = hid if k % 2 == 0 else cur
            for group in (first, rest):
                build_columns(src, k, group, lambda b: b)
                convolve(group)
                epilogue(k, res, dst, group, lambda b: b)
                take_faces(dst, k + 1, group)
                if group is first:
                    make_offer(k + 1)
                    send(k + 1)
            pass_on(k + 1, range(relayed - 2))
            build_weights(k + 1)
            pass_on(k + 1, range(relayed - 2, relayed))
        else:
            for group in (first, rest):
                build_columns(src, k, group, lambda b: inv[b])
                convolve(group)
                epilogue(k, res, out, group, lambda b: inv[b])
    for k in range(convs):
        finish_sends(k)


def shards(nsp, nsl, features, live, rim_slots, neighbours, weights, biases):
    bricks, _, _, width = features.shape
    ch = biases.shape[-1]
    convs, taps, _ = weights.shape
    rims = rim_slots.shape[-1]
    entries = bricks + 4 * rims + 1
    pair = 2 * ch
    rows = ch * ch // pair
    planes = weights.reshape(convs, taps, rows, pair).transpose(1, 2, 0, 3)
    half = width // 2
    kdy = 3 * (half + pair)
    group = max(rims, bricks - rims)
    inner = (SIDE - 2) * pair
    f32, bf16 = jnp.float32, jnp.bfloat16
    smem = pl.BlockSpec(memory_space=pltpu.SMEM)
    vmem = pl.BlockSpec(memory_space=pltpu.VMEM)
    return pl.pallas_call(
        functools.partial(layers_kernel, nsp, nsl),
        out_shape=jax.ShapeDtypeStruct(features.shape, f32),
        in_specs=[smem, smem, smem, vmem, vmem, pl.BlockSpec(memory_space=pl.ANY)],
        out_specs=vmem,
        scratch_shapes=[
            pltpu.VMEM(features.shape, f32),
            pltpu.VMEM(features.shape, f32),
            pltpu.VMEM((convs, rims, 2, SIDE, width), f32),
            pltpu.VMEM((convs, rims, 2, SIDE, width), f32),
            pltpu.VMEM((convs, rims, SIDE, inner), f32),
            pltpu.VMEM((SIDE + 2, 2 * SIDE, width + 2 * pair), f32),
            pltpu.VMEM((SIDE + 2, group * 2 * SIDE, 2 * kdy), bf16),
            pltpu.VMEM((3, 2 * kdy, half), bf16),
            pltpu.VMEM((3, kdy, half), bf16),
            pltpu.VMEM((convs, taps, rows, pair), f32),
            pltpu.VMEM((4, ch, pair), f32),
            pltpu.VMEM((SIDE, group * 2 * SIDE, half), f32),
            pltpu.SMEM((entries,), jnp.int32),
            pltpu.SMEM((bricks,), jnp.int32),
            pltpu.SMEM((bricks,), jnp.int32),
            pltpu.SMEM(neighbours.shape, jnp.int32),
            pltpu.SemaphoreType.DMA((convs,)),
            pltpu.SemaphoreType.DMA((convs, 4, 3 * rims)),
            pltpu.SemaphoreType.DMA((convs, 4, 3 * rims)),
        ]
        + [pltpu.VMEM((entries, 2, SIDE, width), f32) for _ in range(2 * convs)]
        + [pltpu.VMEM((entries, SIDE, inner), f32) for _ in range(convs)],
        compiler_params=pltpu.CompilerParams(
            collective_id=0, has_side_effects=True, vmem_limit_bytes=56 * 1024 * 1024
        ),
        name="layers",
    )(neighbours, live, rim_slots, features, biases, planes)


def solution(mesh):
    in_specs = (
        P(("space", "slab"), None, None, None),
        P(("space", "slab")),
        P(("space", "slab"), None),
        P(("space", "slab"), None),
        P(),
        P(),
    )
    out_specs = P(("space", "slab"), None, None, None)
    body = functools.partial(shards, mesh.shape["space"], mesh.shape["slab"])
    return jax.shard_map(body, mesh=mesh, in_specs=in_specs, out_specs=out_specs, check_vma=False)
```

```python
import functools

import jax
import jax.numpy as jnp
from jax import lax
from jax.experimental import pallas as pl
from jax.experimental.pallas import tpu as pltpu
from jax.sharding import PartitionSpec as P

MESH = pl.DeviceIdType.MESH
SIDE = 8
RELAYED = (3, 3)


def direction_number(dx, dy, dz):
    index = 9 * (dx + 1) + 3 * (dy + 1) + (dz + 1)
    return index if index < 13 else index - 1


def layers_kernel(
    nsp, nsl, nbr, live, rim, f_hbm, b_hbm, w_hbm, out,
    feat, bias, cur, hid, stage, offx, offy, offz, pad, cols, whi, wlo, wbuf, blk, acc,
    emap, inv, perm, nb, isem, osem, wsem, ssem, rsem, *tabs,
):
    bricks = f_hbm.shape[0]
    width = f_hbm.shape[-1]
    ch = width // SIDE
    half = width // 2
    pair = 2 * ch
    ktile = half + pair
    kdy = 3 * ktile
    rims = rim.shape[1]
    convs = w_hbm.shape[2]
    tabx, taby, tabz = tabs[:convs], tabs[convs:2 * convs], tabs[2 * convs:]
    last = bricks + 4 * rims
    sp = lax.axis_index("space")
    sl = lax.axis_index("slab")
    odd = lax.rem(sp, 2)

    near = (sp + 1 - 2 * odd, sl)
    far = (sp - 1 + 2 * odd, sl)
    via = (sp - 2 + 4 * odd, sl)
    onto = (sp + 2 - 4 * odd, sl)
    has_far = jnp.where(odd == 1, sp < nsp - 1, sp > 0)
    has_onto = jnp.where(odd == 1, sp > 1, sp < nsp - 2)
    lower = (sl > 0, (sp, sl - 1))
    upper = (sl < nsl - 1, (sp, sl + 1))
    near_first = bricks + rims * (1 - odd)
    far_first = bricks + rims * odd

    barrier = pltpu.get_barrier_semaphore()
    greeted = ((sp >= 0, near), (has_far, far), (has_far, via), (has_onto, onto), lower, upper)
    for has, peer in greeted:
        @pl.when(has)
        def _():
            pl.semaphore_signal(barrier, inc=1, device_id=peer, device_id_type=MESH)

    def weight_copy(k):
        return pltpu.make_async_copy(w_hbm.at[:, :, k], wbuf.at[k], wsem.at[k])

    feature_copy = pltpu.make_async_copy(f_hbm, feat, isem.at[0])
    bias_copy = pltpu.make_async_copy(b_hbm, bias, isem.at[1])
    feature_copy.start()
    bias_copy.start()
    for k in range(convs):
        weight_copy(k).start()

    def out_copy(b):
        return pltpu.make_async_copy(stage.at[b], out.at[b], osem.at[b])

    chunks = [(j, part) for j in range(rims) for part in range(3)]
    relayed = [min(RELAYED[min(k, 1)], len(chunks)) for k in range(convs)]

    def offered(k, j, part):
        if j == 0:
            return entry_of(k, 0, part)
        if part == 0:
            return offx.at[k, j - 1]
        if part == 1:
            return offy.at[k, j - 1, :, 1:SIDE - 1, :]
        return offz.at[k, j - 1]

    def entry_of(k, at, part):
        if part == 0:
            return tabx[k].at[at]
        if part == 1:
            return taby[k].at[at, :, 1:SIDE - 1, :]
        return tabz[k].at[at]

    def copy(k, src, dst, flow, index, peer):
        return pltpu.make_async_remote_copy(
            src_ref=src, dst_ref=dst, send_sem=ssem.at[k, flow, index],
            recv_sem=rsem.at[k, flow, index], device_id=peer, device_id_type=MESH,
        )

    def to_near(k, c):
        j, part = chunks[c]
        return copy(k, offered(k, j, part), entry_of(k, far_first + j, part), 0, c, near)

    def from_near(k, c):
        j, part = chunks[c]
        return copy(k, offered(k, j, part), entry_of(k, near_first + j, part), 0, c, near)

    def to_far(k, c):
        j, part = chunks[c]
        return copy(k, offered(k, j, part), entry_of(k, near_first + j, part), 1, c, far)

    def relay(k, c):
        j, part = chunks[c]
        return copy(
            k, entry_of(k, near_first + j, part), entry_of(k, far_first + j, part), 1, c, onto
        )

    def from_far(k, c):
        j, part = chunks[c]
        return copy(k, offered(k, j, part), entry_of(k, far_first + j, part), 1, c, far)

    def beside(k, d, j, part, to):
        first = bricks + rims * (d ^ 1 if to else d)
        index = 3 * j + part
        peer = (lower if d == 2 else upper)[1]
        return pltpu.make_async_remote_copy(
            src_ref=offered(k, j, part), dst_ref=entry_of(k, first + j, part),
            send_sem=ssem.at[k, d, index], recv_sem=rsem.at[k, d ^ 1 if to else d, index],
            device_id=peer, device_id_type=MESH,
        )

    def send(k, brick):
        own = range(3 * brick, 3 * brick + 3)
        for c in own:
            if c < relayed[k]:
                to_near(k, c).start()

        for c in own:
            if c >= relayed[k]:
                to_near(k, c).start()

                @pl.when(has_far)
                def _():
                    to_far(k, c).start()
        for d, (has, _) in ((2, lower), (3, upper)):
            @pl.when(has)
            def _():
                for part in range(3):
                    beside(k, d, brick, part, True).start()

    def pass_on(k, some):
        for c in some:
            from_near(k, c).wait_recv()

            @pl.when(has_onto)
            def _():
                relay(k, c).start()

    def receive(k):
        for c in range(relayed[k], len(chunks)):
            from_near(k, c).wait_recv()
        for d, (has, _) in ((2, lower), (3, upper)):
            @pl.when(has)
            def _():
                for j, part in chunks:
                    beside(k, d, j, part, False).wait_recv()

        @pl.when(has_far)
        def _():
            for c in range(len(chunks)):
                from_far(k, c).wait_recv()

    def finish_sends(k):
        for c in range(len(chunks)):
            to_near(k, c).wait_send()

        @pl.when(has_far)
        def _():
            for c in range(relayed[k], len(chunks)):
                to_far(k, c).wait_send()

        @pl.when(has_onto)
        def _():
            for c in range(relayed[k]):
                relay(k, c).wait_send()
        for d, (has, _) in ((2, lower), (3, upper)):
            @pl.when(has)
            def _():
                for j, part in chunks:
                    beside(k, d, j, part, True).wait_send()

    slots = [rim[0, j] for j in range(rims)]
    score = []
    for b in range(bricks):
        s = rims + b
        for j in reversed(range(rims)):
            s = jnp.where(slots[j] == b, j, s)
        score.append(s)
    place = [
        sum(jnp.where(score[o] < score[b], 1, 0) for o in range(bricks) if o != b)
        for b in range(bricks)
    ]
    held = [
        sum(jnp.where(place[b] == p, b, 0) for b in range(bricks)) for p in range(bricks)
    ]
    for b in range(bricks):
        inv[b] = place[b]
        perm[b] = held[b]
    spot = [sum(jnp.where(slots[j] == b, place[b], 0) for b in range(bricks)) for j in range(rims)]

    def mask_of(b):
        return jnp.where(b < live[0, 0], 1.0, 0.0).astype(jnp.float32)

    low = lax.broadcasted_iota(jnp.int32, (SIDE, pair), 1) < ch
    low1 = lax.broadcasted_iota(jnp.int32, (1, pair), 1) < ch
    loww = lax.broadcasted_iota(jnp.int32, wbuf.shape[2:], 1) < ch

    def take_faces(src, k, p):
        tabx[k][p, 0] = src[p, 0]
        tabx[k][p, 1] = src[p, SIDE - 1]
        for s, y in ((0, 0), (1, SIDE - 1)):
            for x in range(1, SIDE - 1):
                taby[k][p, s, x:x + 1, :] = src[p, x, y:y + 1, :]
        for x in range(1, SIDE - 1):
            at = (x - 1) * pair
            tabz[k][p, :, at:at + pair] = jnp.where(
                low, src[p, x, :, 0:pair], src[p, x, :, width - pair:width]
            )

    def offer(k, j):
        if j > 0:
            for off, tab in ((offx, tabx[k]), (offy, taby[k]), (offz, tabz[k])):
                value = tab[0]
                for p in range(1, j + 1):
                    value = jnp.where(spot[j] == p, tab[p], value)
                off[k, j - 1] = value
        send(k, j)

    def build_weights(k):
        weight_copy(k).wait()
        w = k % 2

        def one(t, carry):
            a = t // 3
            base = pl.multiple_of((t - 3 * a) * ktile, ktile)
            taps = [wbuf[k, 3 * t + i] for i in range(3)]
            turned = [pltpu.roll(tap, ch, 1) for tap in taps]
            none = jnp.zeros(taps[0].shape, jnp.float32)
            rows = taps[0].shape[0]
            for j in range(4):
                first, first_turned = (taps[j], turned[j]) if j < 3 else (none, none)
                second, second_turned = (taps[j - 1], turned[j - 1]) if j > 0 else (none, none)
                blk[j, pl.ds(0, rows, stride=2), :] = jnp.where(loww, first, second_turned)
                blk[j, pl.ds(1, rows, stride=2), :] = jnp.where(loww, first_turned, second)
            for j in range(4):
                block = blk[j]
                hi = block.astype(jnp.bfloat16)
                lo = (block - hi.astype(jnp.float32)).astype(jnp.bfloat16)
                for q in range(2):
                    z = j - 1 + 2 * q
                    row = base + (z if z >= 0 else 5) * ch
                    row = pl.multiple_of(row, ch)
                    lanes = slice(q * pair, (q + 1) * pair)
                    whi[w, a, pl.ds(row, ch), lanes] = hi
                    whi[w, a, pl.ds(pl.multiple_of(row + kdy, ch), ch), lanes] = hi
                    wlo[w, a, pl.ds(row, ch), lanes] = lo
            return carry

        lax.fori_loop(0, 9, one, 0)

    def row_of(center, below, above, mask):
        return jnp.concatenate(
            [
                center[:, :half],
                jnp.where(mask, center[:, half:half + pair], below),
                center[:, half:],
                jnp.where(mask, above, center[:, half - pair:half]),
            ],
            axis=1,
        )

    def build_columns(src, k, p, c):
        tx, ty, tz = tabx[k], taby[k], tabz[k]

        def entry(dx, dy, dz):
            return nb[p, direction_number(dx, dy, dz)]

        def x_row(dx, dy, s, y):
            return row_of(
                tx[entry(dx, dy, 0), s, y:y + 1, :],
                tx[entry(dx, dy, -1), s, y:y + 1, width - pair:width],
                tx[entry(dx, dy, 1), s, y:y + 1, 0:pair],
                low1,
            )

        for dx, xrow, s in ((-1, 0, 1), (1, SIDE + 1, 0)):
            pad[xrow, 1:SIDE + 1, :] = row_of(
                tx[entry(dx, 0, 0), s],
                tx[entry(dx, 0, -1), s, :, width - pair:width],
                tx[entry(dx, 0, 1), s, :, 0:pair],
                low,
            )
            for dy, yrow, y in ((-1, 0, SIDE - 1), (1, SIDE + 1, 0)):
                pad[xrow, yrow:yrow + 1, :] = x_row(dx, dy, s, y)
        nlow, nhigh = entry(0, 0, -1), entry(0, 0, 1)
        for x in range(SIDE):
            if x in (0, SIDE - 1):
                s = 0 if x == 0 else 1
                below = tx[nlow, s, :, width - pair:width]
                above = tx[nhigh, s, :, 0:pair]
            else:
                at = (x - 1) * pair
                below = tz[nlow, :, at:at + pair]
                above = tz[nhigh, :, at:at + pair]
            pad[1 + x, 1:SIDE + 1, :] = row_of(src[p, x], below, above, low)
        for dy, yrow, s, y in ((-1, 0, 1, SIDE - 1), (1, SIDE + 1, 0, 0)):
            rows = row_of(
                ty[entry(0, dy, 0), s],
                ty[entry(0, dy, -1), s, :, width - pair:width],
                ty[entry(0, dy, 1), s, :, 0:pair],
                low,
            )
            for x in range(1, SIDE - 1):
                pad[1 + x, yrow:yrow + 1, :] = rows[x:x + 1]
            pad[1, yrow:yrow + 1, :] = x_row(0, dy, 0, y)
            pad[SIDE, yrow:yrow + 1, :] = x_row(0, dy, 1, y)
        for x in range(SIDE + 2):
            for dy in range(3):
                v = pad[x, dy:dy + SIDE, :]
                v = jnp.concatenate([v[:, :ktile], v[:, ktile:]], axis=0)
                hi = v.astype(jnp.bfloat16)
                lo = (v - hi.astype(jnp.float32)).astype(jnp.bfloat16)
                cols[c, x, :, dy * ktile:(dy + 1) * ktile] = hi
                cols[c, x, :, kdy + dy * ktile:kdy + (dy + 1) * ktile] = lo

    def convolve(k, c):
        w = k % 2
        rows = SIDE * 2 * SIDE
        left = [cols[c, a:a + SIDE].reshape(rows, 2 * kdy) for a in range(3)]

        def dot(x, y):
            return jnp.dot(x, y, preferred_element_type=jnp.float32)

        tile = 2 * pair
        tiles = -(-2 * kdy // tile) + -(-kdy // tile)
        cut = (tiles // 2) * tile
        one = dot(left[0], whi[w, 0]) + dot(left[0][:, :kdy], wlo[w, 0])
        one = one + dot(left[1][:, :cut], whi[w, 1, :cut])
        two = dot(left[2], whi[w, 2]) + dot(left[2][:, :kdy], wlo[w, 2])
        two = two + dot(left[1][:, cut:], whi[w, 1, cut:]) + dot(left[1][:, :kdy], wlo[w, 1])
        acc[odd] = one
        acc[1 - odd] = two

    def epilogue(k, res, dst, p, at, m):
        bvec = bias[k:k + 1, :]
        bvec = jnp.concatenate([bvec, bvec, bvec, bvec], axis=1)
        for x in range(SIDE):
            for t in range(2):
                row = (2 * x + t) * SIDE
                v = acc[0, row:row + SIDE, :] + acc[1, row:row + SIDE, :] + bvec
                lanes = slice(t * half, (t + 1) * half)
                if res is not None:
                    v = v + res[p, x, :, lanes]
                dst[at, x, :, lanes] = jnp.maximum(v, 0.0) * m

    def mask_features(p, carry):
        cur[p] = feat[perm[p]] * mask_of(perm[p])
        return carry

    feature_copy.wait()
    lax.fori_loop(0, bricks, mask_features, 0)
    for p in range(rims):
        take_faces(cur, 0, p)
    arrivals = sum(jnp.where(has, 1, 0) for has, _ in greeted)
    pl.semaphore_wait(barrier, arrivals)
    for j in range(rims):
        offer(0, j)

    for p in range(rims, bricks):
        take_faces(cur, 0, p)
    for k in range(convs):
        for tab in (tabx[k], taby[k], tabz[k]):
            tab[last] = jnp.zeros(tab.shape[1:], jnp.float32)
    for e in range(last + 1):
        if e < bricks:
            emap[e] = place[e]
        elif e < bricks + rims:
            emap[e] = jnp.where(sp > 0, e, last)
        elif e < bricks + 2 * rims:
            emap[e] = jnp.where(sp < nsp - 1, e, last)
        elif e < bricks + 3 * rims:
            emap[e] = jnp.where(sl > 0, e, last)
        elif e < last:
            emap[e] = jnp.where(sl < nsl - 1, e, last)
        else:
            emap[e] = last

    def remap(j, carry):
        for p in range(bricks):
            nb[p, j] = emap[nbr[perm[p], j]]
        return carry

    lax.fori_loop(0, nbr.shape[1], remap, 0)
    whi[...] = jnp.zeros_like(whi)
    wlo[...] = jnp.zeros_like(wlo)
    build_weights(0)
    bias_copy.wait()
    pass_on(0, range(relayed[0]))

    for k in range(convs):
        src = cur if k % 2 == 0 else hid
        res = None if k % 2 == 0 else cur
        receive(k)
        end = k == convs - 1
        if end:
            dst = stage
            spots = [inv[b] for b in range(bricks)]
        else:
            dst = hid if k % 2 == 0 else cur
            spots = list(range(bricks))
        waiting = [] if end else list(range(relayed[k + 1]))
        build_columns(src, k, spots[0], 0)
        for i in range(bricks):
            p = spots[i]
            if i + 1 < bricks and (end or i != 0):
                build_columns(src, k, spots[i + 1], (i + 1) % 2)
            convolve(k, i % 2)
            if end:
                epilogue(k, res, dst, p, i, mask_of(i))
                out_copy(i).start()
                continue
            epilogue(k, res, dst, p, i, mask_of(perm[i]))
            take_faces(dst, k + 1, i)
            if i < rims:
                offer(k + 1, i)
                if i == 0 and bricks > 1:
                    build_columns(src, k, spots[1], 1)
            elif i == rims:
                pass_on(k + 1, waiting[:1])
                build_weights(k + 1)
                pass_on(k + 1, waiting[1:3])
                waiting = waiting[3:]
        if not end:
            pass_on(k + 1, waiting)
    for b in range(bricks):
        out_copy(b).wait()
    for k in range(convs):
        finish_sends(k)


def shards(nsp, nsl, features, live, rim_slots, neighbours, weights, biases):
    bricks, _, _, width = features.shape
    ch = biases.shape[-1]
    convs, taps, _ = weights.shape
    rims = rim_slots.shape[-1]
    entries = bricks + 4 * rims + 1
    pair = 2 * ch
    rows = ch * ch // pair
    planes = weights.reshape(convs, taps, rows, pair).transpose(1, 2, 0, 3)
    half = width // 2
    kdy = 3 * (half + pair)
    inner = (SIDE - 2) * pair
    f32, bf16 = jnp.float32, jnp.bfloat16
    smem = pl.BlockSpec(memory_space=pltpu.SMEM)
    hbm = pl.BlockSpec(memory_space=pl.ANY)
    return pl.pallas_call(
        functools.partial(layers_kernel, nsp, nsl),
        out_shape=jax.ShapeDtypeStruct(features.shape, f32),
        in_specs=[smem, smem, smem, hbm, hbm, hbm],
        out_specs=hbm,
        scratch_shapes=[
            pltpu.VMEM(features.shape, f32),
            pltpu.VMEM(biases.shape, f32),
            pltpu.VMEM(features.shape, f32),
            pltpu.VMEM(features.shape, f32),
            pltpu.VMEM(features.shape, f32),
            pltpu.VMEM((convs, max(rims - 1, 1), 2, SIDE, width), f32),
            pltpu.VMEM((convs, max(rims - 1, 1), 2, SIDE, width), f32),
            pltpu.VMEM((convs, max(rims - 1, 1), SIDE, inner), f32),
            pltpu.VMEM((SIDE + 2, 2 * SIDE, width + 2 * pair), f32),
            pltpu.VMEM((2, SIDE + 2, 2 * SIDE, 2 * kdy), bf16),
            pltpu.VMEM((2, 3, 2 * kdy, half), bf16),
            pltpu.VMEM((2, 3, kdy, half), bf16),
            pltpu.VMEM((convs, taps, rows, pair), f32),
            pltpu.VMEM((4, ch, pair), f32),
            pltpu.VMEM((2, SIDE * 2 * SIDE, half), f32),
            pltpu.SMEM((entries,), jnp.int32),
            pltpu.SMEM((bricks,), jnp.int32),
            pltpu.SMEM((bricks,), jnp.int32),
            pltpu.SMEM(neighbours.shape, jnp.int32),
            pltpu.SemaphoreType.DMA((2,)),
            pltpu.SemaphoreType.DMA((bricks,)),
            pltpu.SemaphoreType.DMA((convs,)),
            pltpu.SemaphoreType.DMA((convs, 4, 3 * rims)),
            pltpu.SemaphoreType.DMA((convs, 4, 3 * rims)),
        ]
        + [pltpu.VMEM((entries, 2, SIDE, width), f32) for _ in range(2 * convs)]
        + [pltpu.VMEM((entries, SIDE, inner), f32) for _ in range(convs)],
        compiler_params=pltpu.CompilerParams(
            collective_id=0, has_side_effects=True, vmem_limit_bytes=56 * 1024 * 1024
        ),
        name="layers",
    )(neighbours, live.reshape(1, 1), rim_slots, features, biases, planes)


def solution(mesh):
    in_specs = (
        P(("space", "slab"), None, None, None),
        P(("space", "slab")),
        P(("space", "slab"), None),
        P(("space", "slab"), None),
        P(),
        P(),
    )
    out_specs = P(("space", "slab"), None, None, None)
    body = functools.partial(shards, mesh.shape["space"], mesh.shape["slab"])
    return jax.shard_map(body, mesh=mesh, in_specs=in_specs, out_specs=out_specs, check_vma=False)
```

```python
import functools

import jax
import jax.numpy as jnp
from jax import lax
from jax.experimental import pallas as pl
from jax.experimental.pallas import tpu as pltpu
from jax.sharding import PartitionSpec as P

MESH = pl.DeviceIdType.MESH
SIDE = 8
RELAYED = (3, 3)


def direction_number(dx, dy, dz):
    index = 9 * (dx + 1) + 3 * (dy + 1) + (dz + 1)
    return index if index < 13 else index - 1


def layers_kernel(
    nsp, nsl, nbr_hbm, live_hbm, rim_hbm, f_hbm, b_hbm, w_hbm, out,
    feat, bias, cur, hid, stage, offx, offy, offz, pad, cols, whi, wlo, wbuf, blk, acc,
    nbr, live, rim, emap, inv, perm, nb, isem, osem, wsem, ssem, rsem, *tabs,
):
    bricks = f_hbm.shape[0]
    width = f_hbm.shape[-1]
    ch = width // SIDE
    half = width // 2
    pair = 2 * ch
    ktile = half + pair
    kdy = 3 * ktile
    rims = rim_hbm.shape[1]
    convs = w_hbm.shape[2]
    tabx, taby, tabz = tabs[:convs], tabs[convs:2 * convs], tabs[2 * convs:]
    last = bricks + 4 * rims
    sp = lax.axis_index("space")
    sl = lax.axis_index("slab")
    odd = lax.rem(sp, 2)

    near = (sp + 1 - 2 * odd, sl)
    far = (sp - 1 + 2 * odd, sl)
    via = (sp - 2 + 4 * odd, sl)
    onto = (sp + 2 - 4 * odd, sl)
    has_far = jnp.where(odd == 1, sp < nsp - 1, sp > 0)
    has_onto = jnp.where(odd == 1, sp > 1, sp < nsp - 2)
    lower = (sl > 0, (sp, sl - 1))
    upper = (sl < nsl - 1, (sp, sl + 1))
    near_first = bricks + rims * (1 - odd)
    far_first = bricks + rims * odd

    barrier = pltpu.get_barrier_semaphore()
    greeted = ((sp >= 0, near), (has_far, far), (has_far, via), (has_onto, onto), lower, upper)
    for has, peer in greeted:
        @pl.when(has)
        def _():
            pl.semaphore_signal(barrier, inc=1, device_id=peer, device_id_type=MESH)

    def weight_copy(k):
        return pltpu.make_async_copy(w_hbm.at[:, :, k], wbuf.at[k], wsem.at[k])

    feature_copy = pltpu.make_async_copy(f_hbm, feat, isem.at[0])
    bias_copy = pltpu.make_async_copy(b_hbm, bias, isem.at[1])
    index_copies = [
        pltpu.make_async_copy(a, b, isem.at[2 + i])
        for i, (a, b) in enumerate(((rim_hbm, rim), (live_hbm, live), (nbr_hbm, nbr)))
    ]
    feature_copy.start()
    for index_copy in index_copies:
        index_copy.start()
    bias_copy.start()
    for k in range(convs):
        weight_copy(k).start()

    def out_copy(b):
        return pltpu.make_async_copy(stage.at[b], out.at[b], osem.at[b])

    chunks = [(j, part) for j in range(rims) for part in range(3)]
    relayed = [min(RELAYED[min(k, 1)], len(chunks)) for k in range(convs)]

    def offered(k, j, part):
        if j == 0:
            return entry_of(k, 0, part)
        if part == 0:
            return offx.at[k, j - 1]
        if part == 1:
            return offy.at[k, j - 1, :, 1:SIDE - 1, :]
        return offz.at[k, j - 1, 1:SIDE - 1, :]

    def entry_of(k, at, part):
        if part == 0:
            return tabx[k].at[at]
        if part == 1:
            return taby[k].at[at, :, 1:SIDE - 1, :]
        return tabz[k].at[at, 1:SIDE - 1, :]

    def copy(k, src, dst, flow, index, peer):
        return pltpu.make_async_remote_copy(
            src_ref=src, dst_ref=dst, send_sem=ssem.at[k, flow, index],
            recv_sem=rsem.at[k, flow, index], device_id=peer, device_id_type=MESH,
        )

    def to_near(k, c):
        j, part = chunks[c]
        return copy(k, offered(k, j, part), entry_of(k, far_first + j, part), 0, c, near)

    def from_near(k, c):
        j, part = chunks[c]
        return copy(k, offered(k, j, part), entry_of(k, near_first + j, part), 0, c, near)

    def to_far(k, c):
        j, part = chunks[c]
        return copy(k, offered(k, j, part), entry_of(k, near_first + j, part), 1, c, far)

    def relay(k, c):
        j, part = chunks[c]
        return copy(
            k, entry_of(k, near_first + j, part), entry_of(k, far_first + j, part), 1, c, onto
        )

    def from_far(k, c):
        j, part = chunks[c]
        return copy(k, offered(k, j, part), entry_of(k, far_first + j, part), 1, c, far)

    def beside(k, d, j, part, to):
        first = bricks + rims * (d ^ 1 if to else d)
        index = 3 * j + part
        peer = (lower if d == 2 else upper)[1]
        return pltpu.make_async_remote_copy(
            src_ref=offered(k, j, part), dst_ref=entry_of(k, first + j, part),
            send_sem=ssem.at[k, d, index], recv_sem=rsem.at[k, d ^ 1 if to else d, index],
            device_id=peer, device_id_type=MESH,
        )

    def send(k, brick):
        own = range(3 * brick, 3 * brick + 3)
        for c in own:
            if c < relayed[k]:
                to_near(k, c).start()

        for c in own:
            if c >= relayed[k]:
                to_near(k, c).start()

                @pl.when(has_far)
                def _():
                    to_far(k, c).start()
        for d, (has, _) in ((2, lower), (3, upper)):
            @pl.when(has)
            def _():
                for part in range(3):
                    beside(k, d, brick, part, True).start()

    def pass_on(k, some):
        for c in some:
            from_near(k, c).wait_recv()

            @pl.when(has_onto)
            def _():
                relay(k, c).start()

    def receive(k):
        for c in range(relayed[k], len(chunks)):
            from_near(k, c).wait_recv()
        for d, (has, _) in ((2, lower), (3, upper)):
            @pl.when(has)
            def _():
                for j, part in chunks:
                    beside(k, d, j, part, False).wait_recv()

        @pl.when(has_far)
        def _():
            for c in range(len(chunks)):
                from_far(k, c).wait_recv()

    def finish_sends(k):
        for c in range(len(chunks)):
            to_near(k, c).wait_send()

        @pl.when(has_far)
        def _():
            for c in range(relayed[k], len(chunks)):
                to_far(k, c).wait_send()

        @pl.when(has_onto)
        def _():
            for c in range(relayed[k]):
                relay(k, c).wait_send()
        for d, (has, _) in ((2, lower), (3, upper)):
            @pl.when(has)
            def _():
                for j, part in chunks:
                    beside(k, d, j, part, True).wait_send()

    for index_copy in index_copies:
        index_copy.wait()

    slots = [rim[0, j] for j in range(rims)]
    score = []
    for b in range(bricks):
        s = rims + b
        for j in reversed(range(rims)):
            s = jnp.where(slots[j] == b, j, s)
        score.append(s)
    place = [
        sum(jnp.where(score[o] < score[b], 1, 0) for o in range(bricks) if o != b)
        for b in range(bricks)
    ]
    held = [
        sum(jnp.where(place[b] == p, b, 0) for b in range(bricks)) for p in range(bricks)
    ]
    for b in range(bricks):
        inv[b] = place[b]
        perm[b] = held[b]
    spot = [sum(jnp.where(slots[j] == b, place[b], 0) for b in range(bricks)) for j in range(rims)]

    def mask_of(b):
        return jnp.where(b < live[0], 1.0, 0.0).astype(jnp.float32)

    low = lax.broadcasted_iota(jnp.int32, (SIDE, pair), 1) < ch
    low1 = lax.broadcasted_iota(jnp.int32, (1, pair), 1) < ch
    loww = lax.broadcasted_iota(jnp.int32, wbuf.shape[2:], 1) < ch

    def take_faces(src, k, p):
        tabx[k][p, 0] = src[p, 0]
        tabx[k][p, 1] = src[p, SIDE - 1]
        for s, y in ((0, 0), (1, SIDE - 1)):
            for x in range(1, SIDE - 1):
                taby[k][p, s, x:x + 1, :] = src[p, x, y:y + 1, :]
        for x in range(1, SIDE - 1):
            at = (x - 1) * pair
            tabz[k][p, :, at:at + pair] = jnp.where(
                low, src[p, x, :, 0:pair], src[p, x, :, width - pair:width]
            )

    def offer(k, j):
        if j > 0:
            for off, tab in ((offx, tabx[k]), (offy, taby[k]), (offz, tabz[k])):
                value = tab[0]
                for p in range(1, j + 1):
                    value = jnp.where(spot[j] == p, tab[p], value)
                off[k, j - 1] = value
        send(k, j)

    def build_weights(k):
        weight_copy(k).wait()
        w = k % 2

        def one(t, carry):
            a = t // 3
            base = pl.multiple_of((t - 3 * a) * ktile, ktile)
            taps = [wbuf[k, 3 * t + i] for i in range(3)]
            turned = [pltpu.roll(tap, ch, 1) for tap in taps]
            none = jnp.zeros(taps[0].shape, jnp.float32)
            rows = taps[0].shape[0]
            for j in range(4):
                first, first_turned = (taps[j], turned[j]) if j < 3 else (none, none)
                second, second_turned = (taps[j - 1], turned[j - 1]) if j > 0 else (none, none)
                blk[j, pl.ds(0, rows, stride=2), :] = jnp.where(loww, first, second_turned)
                blk[j, pl.ds(1, rows, stride=2), :] = jnp.where(loww, first_turned, second)
            for j in range(4):
                block = blk[j]
                hi = block.astype(jnp.bfloat16)
                lo = (block - hi.astype(jnp.float32)).astype(jnp.bfloat16)
                for q in range(2):
                    z = j - 1 + 2 * q
                    row = base + (z if z >= 0 else 5) * ch
                    row = pl.multiple_of(row, ch)
                    lanes = slice(q * pair, (q + 1) * pair)
                    whi[w, a, pl.ds(row, ch), lanes] = hi
                    whi[w, a, pl.ds(pl.multiple_of(row + kdy, ch), ch), lanes] = hi
                    wlo[w, a, pl.ds(row, ch), lanes] = lo
            return carry

        lax.fori_loop(0, 9, one, 0)

    def row_of(center, below, above, mask):
        return jnp.concatenate(
            [
                center[:, :half],
                jnp.where(mask, center[:, half:half + pair], below),
                center[:, half:],
                jnp.where(mask, above, center[:, half - pair:half]),
            ],
            axis=1,
        )

    def build_columns(src, k, p, c):
        tx, ty, tz = tabx[k], taby[k], tabz[k]

        def entry(dx, dy, dz):
            return nb[p, direction_number(dx, dy, dz)]

        def x_row(dx, dy, s, y):
            return row_of(
                tx[entry(dx, dy, 0), s, y:y + 1, :],
                tx[entry(dx, dy, -1), s, y:y + 1, width - pair:width],
                tx[entry(dx, dy, 1), s, y:y + 1, 0:pair],
                low1,
            )

        for dx, xrow, s in ((-1, 0, 1), (1, SIDE + 1, 0)):
            pad[xrow, 1:SIDE + 1, :] = row_of(
                tx[entry(dx, 0, 0), s],
                tx[entry(dx, 0, -1), s, :, width - pair:width],
                tx[entry(dx, 0, 1), s, :, 0:pair],
                low,
            )
            for dy, yrow, y in ((-1, 0, SIDE - 1), (1, SIDE + 1, 0)):
                pad[xrow, yrow:yrow + 1, :] = x_row(dx, dy, s, y)
        nlow, nhigh = entry(0, 0, -1), entry(0, 0, 1)
        for x in range(SIDE):
            if x in (0, SIDE - 1):
                s = 0 if x == 0 else 1
                below = tx[nlow, s, :, width - pair:width]
                above = tx[nhigh, s, :, 0:pair]
            else:
                at = (x - 1) * pair
                below = tz[nlow, :, at:at + pair]
                above = tz[nhigh, :, at:at + pair]
            pad[1 + x, 1:SIDE + 1, :] = row_of(src[p, x], below, above, low)
            if 0 < x < SIDE - 1:
                for s, y in ((0, 0), (1, SIDE - 1)):
                    row = slice(1 + y, 2 + y)
                    pad[1 + x, row, half:half + pair] = jnp.where(
                        low1, src[p, x, y:y + 1, half:half + pair],
                        ty[nlow, s, x:x + 1, width - pair:width],
                    )
                    pad[1 + x, row, width + pair:width + 2 * pair] = jnp.where(
                        low1, ty[nhigh, s, x:x + 1, 0:pair],
                        src[p, x, y:y + 1, half - pair:half],
                    )
        for dy, yrow, s, y in ((-1, 0, 1, SIDE - 1), (1, SIDE + 1, 0, 0)):
            rows = row_of(
                ty[entry(0, dy, 0), s],
                ty[entry(0, dy, -1), s, :, width - pair:width],
                ty[entry(0, dy, 1), s, :, 0:pair],
                low,
            )
            for x in range(1, SIDE - 1):
                pad[1 + x, yrow:yrow + 1, :] = rows[x:x + 1]
            pad[1, yrow:yrow + 1, :] = x_row(0, dy, 0, y)
            pad[SIDE, yrow:yrow + 1, :] = x_row(0, dy, 1, y)
        for x in range(SIDE + 2):
            for dy in range(3):
                v = pad[x, dy:dy + SIDE, :]
                v = jnp.concatenate([v[:, :ktile], v[:, ktile:]], axis=0)
                hi = v.astype(jnp.bfloat16)
                lo = (v - hi.astype(jnp.float32)).astype(jnp.bfloat16)
                cols[c, x, :, dy * ktile:(dy + 1) * ktile] = hi
                cols[c, x, :, kdy + dy * ktile:kdy + (dy + 1) * ktile] = lo

    def convolve(k, c):
        w = k % 2
        rows = SIDE * 2 * SIDE
        left = [cols[c, a:a + SIDE].reshape(rows, 2 * kdy) for a in range(3)]

        def dot(x, y):
            return jnp.dot(x, y, preferred_element_type=jnp.float32)

        tile = 2 * pair
        tiles = -(-2 * kdy // tile) + -(-kdy // tile)
        cut = (tiles // 2) * tile
        one = dot(left[0], whi[w, 0]) + dot(left[0][:, :kdy], wlo[w, 0])
        one = one + dot(left[1][:, :cut], whi[w, 1, :cut])
        two = dot(left[2], whi[w, 2]) + dot(left[2][:, :kdy], wlo[w, 2])
        two = two + dot(left[1][:, cut:], whi[w, 1, cut:]) + dot(left[1][:, :kdy], wlo[w, 1])
        acc[odd] = one
        acc[1 - odd] = two

    def epilogue(k, res, dst, p, at, m):
        bvec = bias[k:k + 1, :]
        bvec = jnp.concatenate([bvec, bvec, bvec, bvec], axis=1)
        for x in range(SIDE):
            for t in range(2):
                row = (2 * x + t) * SIDE
                v = acc[0, row:row + SIDE, :] + acc[1, row:row + SIDE, :] + bvec
                lanes = slice(t * half, (t + 1) * half)
                if res is not None:
                    v = v + res[p, x, :, lanes]
                dst[at, x, :, lanes] = jnp.maximum(v, 0.0) * m

    def mask_features(p, carry):
        cur[p] = feat[perm[p]] * mask_of(perm[p])
        return carry

    feature_copy.wait()
    lax.fori_loop(0, bricks, mask_features, 0)
    for p in range(rims):
        take_faces(cur, 0, p)
    arrivals = sum(jnp.where(has, 1, 0) for has, _ in greeted)
    pl.semaphore_wait(barrier, arrivals)
    for j in range(rims):
        offer(0, j)

    for p in range(rims, bricks):
        take_faces(cur, 0, p)
    for k in range(convs):
        for tab in (tabx[k], taby[k], tabz[k]):
            tab[last] = jnp.zeros(tab.shape[1:], jnp.float32)
    for e in range(last + 1):
        if e < bricks:
            emap[e] = place[e]
        elif e < bricks + rims:
            emap[e] = jnp.where(sp > 0, e, last)
        elif e < bricks + 2 * rims:
            emap[e] = jnp.where(sp < nsp - 1, e, last)
        elif e < bricks + 3 * rims:
            emap[e] = jnp.where(sl > 0, e, last)
        elif e < last:
            emap[e] = jnp.where(sl < nsl - 1, e, last)
        else:
            emap[e] = last

    def remap(j, carry):
        for p in range(bricks):
            nb[p, j] = emap[nbr[perm[p], j]]
        return carry

    lax.fori_loop(0, nbr.shape[1], remap, 0)
    whi[...] = jnp.zeros_like(whi)
    wlo[...] = jnp.zeros_like(wlo)
    build_weights(0)
    bias_copy.wait()
    pass_on(0, range(relayed[0]))

    for k in range(convs):
        src = cur if k % 2 == 0 else hid
        res = None if k % 2 == 0 else cur
        receive(k)
        end = k == convs - 1
        if end:
            dst = stage
            spots = [inv[b] for b in range(bricks)]
        else:
            dst = hid if k % 2 == 0 else cur
            spots = list(range(bricks))
        waiting = [] if end else list(range(relayed[k + 1]))
        build_columns(src, k, spots[0], 0)
        for i in range(bricks):
            p = spots[i]
            if i + 1 < bricks and (end or i != 0):
                build_columns(src, k, spots[i + 1], (i + 1) % 2)
            convolve(k, i % 2)
            if end:
                epilogue(k, res, dst, p, i, mask_of(i))
                out_copy(i).start()
                continue
            epilogue(k, res, dst, p, i, mask_of(perm[i]))
            take_faces(dst, k + 1, i)
            if i < rims:
                offer(k + 1, i)
                if i == 0 and bricks > 1:
                    build_columns(src, k, spots[1], 1)
            elif i == rims:
                pass_on(k + 1, waiting[:1])
                build_weights(k + 1)
                pass_on(k + 1, waiting[1:3])
                waiting = waiting[3:]
        if not end:
            pass_on(k + 1, waiting)
    for b in range(bricks):
        out_copy(b).wait()
    for k in range(convs):
        finish_sends(k)


def shards(nsp, nsl, features, live, rim_slots, neighbours, weights, biases):
    bricks, _, _, width = features.shape
    ch = biases.shape[-1]
    convs, taps, _ = weights.shape
    rims = rim_slots.shape[-1]
    entries = bricks + 4 * rims + 1
    pair = 2 * ch
    rows = ch * ch // pair
    planes = weights.reshape(convs, taps, rows, pair).transpose(1, 2, 0, 3)
    half = width // 2
    kdy = 3 * (half + pair)
    inner = (SIDE - 2) * pair
    f32, bf16 = jnp.float32, jnp.bfloat16
    hbm = pl.BlockSpec(memory_space=pltpu.HBM)
    def far(a):
        return pltpu.with_memory_space_constraint(a, pltpu.HBM)

    return pl.pallas_call(
        functools.partial(layers_kernel, nsp, nsl),
        out_shape=jax.ShapeDtypeStruct(features.shape, f32),
        in_specs=[hbm] * 6,
        out_specs=pl.BlockSpec(memory_space=pl.ANY),
        scratch_shapes=[
            pltpu.VMEM(features.shape, f32),
            pltpu.VMEM(biases.shape, f32),
            pltpu.VMEM(features.shape, f32),
            pltpu.VMEM(features.shape, f32),
            pltpu.VMEM(features.shape, f32),
            pltpu.VMEM((convs, max(rims - 1, 1), 2, SIDE, width), f32),
            pltpu.VMEM((convs, max(rims - 1, 1), 2, SIDE, width), f32),
            pltpu.VMEM((convs, max(rims - 1, 1), SIDE, inner), f32),
            pltpu.VMEM((SIDE + 2, 2 * SIDE, width + 2 * pair), f32),
            pltpu.VMEM((2, SIDE + 2, 2 * SIDE, 2 * kdy), bf16),
            pltpu.VMEM((2, 3, 2 * kdy, half), bf16),
            pltpu.VMEM((2, 3, kdy, half), bf16),
            pltpu.VMEM((convs, taps, rows, pair), f32),
            pltpu.VMEM((4, ch, pair), f32),
            pltpu.VMEM((2, SIDE * 2 * SIDE, half), f32),
            pltpu.SMEM(neighbours.shape, jnp.int32),
            pltpu.SMEM(live.shape, jnp.int32),
            pltpu.SMEM(rim_slots.shape, jnp.int32),
            pltpu.SMEM((entries,), jnp.int32),
            pltpu.SMEM((bricks,), jnp.int32),
            pltpu.SMEM((bricks,), jnp.int32),
            pltpu.SMEM(neighbours.shape, jnp.int32),
            pltpu.SemaphoreType.DMA((5,)),
            pltpu.SemaphoreType.DMA((bricks,)),
            pltpu.SemaphoreType.DMA((convs,)),
            pltpu.SemaphoreType.DMA((convs, 4, 3 * rims)),
            pltpu.SemaphoreType.DMA((convs, 4, 3 * rims)),
        ]
        + [pltpu.VMEM((entries, 2, SIDE, width), f32) for _ in range(2 * convs)]
        + [pltpu.VMEM((entries, SIDE, inner), f32) for _ in range(convs)],
        compiler_params=pltpu.CompilerParams(
            collective_id=0, has_side_effects=True, vmem_limit_bytes=26 * 1024 * 1024
        ),
        name="layers",
    )(far(neighbours), live, far(rim_slots), far(features), far(biases), far(planes))


def solution(mesh):
    in_specs = (
        P(("space", "slab"), None, None, None),
        P(("space", "slab")),
        P(("space", "slab"), None),
        P(("space", "slab"), None),
        P(),
        P(),
    )
    out_specs = P(("space", "slab"), None, None, None)
    body = functools.partial(shards, mesh.shape["space"], mesh.shape["slab"])
    return jax.shard_map(body, mesh=mesh, in_specs=in_specs, out_specs=out_specs, check_vma=False)
```

```python
import functools

import jax
import jax.numpy as jnp
from jax import lax
from jax.experimental import pallas as pl
from jax.experimental.pallas import tpu as pltpu
from jax.sharding import PartitionSpec as P

MESH = pl.DeviceIdType.MESH
SIDE = 8
RELAYED = (3, 2)


def direction_number(dx, dy, dz):
    index = 9 * (dx + 1) + 3 * (dy + 1) + (dz + 1)
    return index if index < 13 else index - 1


def layers_kernel(
    nsp, nsl, nbr_hbm, live_hbm, rim_hbm, f_hbm, b_hbm, w_hbm, out,
    feat, bias, cur, hid, stage, offx, offy, offz, pad, cols, whi, wlo, wbuf, blk, acc,
    nbr, live, rim, emap, inv, perm, nb, isem, osem, wsem, ssem, rsem, *tabs,
):
    bricks = f_hbm.shape[0]
    width = f_hbm.shape[-1]
    ch = width // SIDE
    half = width // 2
    pair = 2 * ch
    ktile = half + pair
    kdy = 3 * ktile
    rims = rim_hbm.shape[1]
    convs = w_hbm.shape[2]
    tabx, taby, tabz = tabs[:convs], tabs[convs:2 * convs], tabs[2 * convs:]
    last = bricks + 4 * rims
    sp = lax.axis_index("space")
    sl = lax.axis_index("slab")
    odd = lax.rem(sp, 2)

    near = (sp + 1 - 2 * odd, sl)
    far = (sp - 1 + 2 * odd, sl)
    via = (sp - 2 + 4 * odd, sl)
    onto = (sp + 2 - 4 * odd, sl)
    has_far = jnp.where(odd == 1, sp < nsp - 1, sp > 0)
    has_onto = jnp.where(odd == 1, sp > 1, sp < nsp - 2)
    lower = (sl > 0, (sp, sl - 1))
    upper = (sl < nsl - 1, (sp, sl + 1))
    near_first = bricks + rims * (1 - odd)
    far_first = bricks + rims * odd

    barrier = pltpu.get_barrier_semaphore()
    greeted = ((sp >= 0, near), (has_far, far), (has_far, via), (has_onto, onto), lower, upper)
    for has, peer in greeted:
        @pl.when(has)
        def _():
            pl.semaphore_signal(barrier, inc=1, device_id=peer, device_id_type=MESH)

    def weight_copy(k):
        return pltpu.make_async_copy(w_hbm.at[:, :, k], wbuf.at[k], wsem.at[k])

    feature_copy = pltpu.make_async_copy(f_hbm, feat, isem.at[0])
    bias_copy = pltpu.make_async_copy(b_hbm, bias, isem.at[1])
    index_copies = [
        pltpu.make_async_copy(a, b, isem.at[2 + i])
        for i, (a, b) in enumerate(((rim_hbm, rim), (live_hbm, live), (nbr_hbm, nbr)))
    ]
    feature_copy.start()
    for index_copy in index_copies:
        index_copy.start()
    bias_copy.start()
    for k in range(convs):
        weight_copy(k).start()

    def out_copy(b):
        return pltpu.make_async_copy(stage.at[b], out.at[b], osem.at[b])

    chunks = [(j, part) for j in range(rims) for part in range(3)]
    relayed = [min(RELAYED[min(k, 1)], len(chunks)) for k in range(convs)]

    def offered(k, j, part):
        if j == 0:
            return entry_of(k, 0, part)
        if part == 0:
            return offx.at[k, j - 1]
        if part == 1:
            return offy.at[k, j - 1, :, 1:SIDE - 1, :]
        return offz.at[k, j - 1, 1:SIDE - 1, :]

    def entry_of(k, at, part):
        if part == 0:
            return tabx[k].at[at]
        if part == 1:
            return taby[k].at[at, :, 1:SIDE - 1, :]
        return tabz[k].at[at, 1:SIDE - 1, :]

    def copy(k, src, dst, flow, index, peer):
        return pltpu.make_async_remote_copy(
            src_ref=src, dst_ref=dst, send_sem=ssem.at[k, flow, index],
            recv_sem=rsem.at[k, flow, index], device_id=peer, device_id_type=MESH,
        )

    def to_near(k, c):
        j, part = chunks[c]
        return copy(k, offered(k, j, part), entry_of(k, far_first + j, part), 0, c, near)

    def from_near(k, c):
        j, part = chunks[c]
        return copy(k, offered(k, j, part), entry_of(k, near_first + j, part), 0, c, near)

    def to_far(k, c):
        j, part = chunks[c]
        return copy(k, offered(k, j, part), entry_of(k, near_first + j, part), 1, c, far)

    def relay(k, c):
        j, part = chunks[c]
        return copy(
            k, entry_of(k, near_first + j, part), entry_of(k, far_first + j, part), 1, c, onto
        )

    def from_far(k, c):
        j, part = chunks[c]
        return copy(k, offered(k, j, part), entry_of(k, far_first + j, part), 1, c, far)

    def beside(k, d, j, part, to):
        first = bricks + rims * (d ^ 1 if to else d)
        index = 3 * j + part
        peer = (lower if d == 2 else upper)[1]
        return pltpu.make_async_remote_copy(
            src_ref=offered(k, j, part), dst_ref=entry_of(k, first + j, part),
            send_sem=ssem.at[k, d, index], recv_sem=rsem.at[k, d ^ 1 if to else d, index],
            device_id=peer, device_id_type=MESH,
        )

    def send(k, brick):
        own = range(3 * brick, 3 * brick + 3)
        for c in own:
            if c < relayed[k]:
                to_near(k, c).start()

        for c in own:
            if c >= relayed[k]:
                to_near(k, c).start()

                @pl.when(has_far)
                def _():
                    to_far(k, c).start()
        for d, (has, _) in ((2, lower), (3, upper)):
            @pl.when(has)
            def _():
                for part in range(3):
                    beside(k, d, brick, part, True).start()

    def pass_on(k, some):
        for c in some:
            from_near(k, c).wait_recv()

            @pl.when(has_onto)
            def _():
                relay(k, c).start()

    def receive(k):
        for c in range(relayed[k], len(chunks)):
            from_near(k, c).wait_recv()
        for d, (has, _) in ((2, lower), (3, upper)):
            @pl.when(has)
            def _():
                for j, part in chunks:
                    beside(k, d, j, part, False).wait_recv()

        @pl.when(has_far)
        def _():
            for c in range(len(chunks)):
                from_far(k, c).wait_recv()

    def finish_sends(k):
        for c in range(len(chunks)):
            to_near(k, c).wait_send()

        @pl.when(has_far)
        def _():
            for c in range(relayed[k], len(chunks)):
                to_far(k, c).wait_send()

        @pl.when(has_onto)
        def _():
            for c in range(relayed[k]):
                relay(k, c).wait_send()
        for d, (has, _) in ((2, lower), (3, upper)):
            @pl.when(has)
            def _():
                for j, part in chunks:
                    beside(k, d, j, part, True).wait_send()

    for index_copy in index_copies:
        index_copy.wait()

    slots = [rim[0, j] for j in range(rims)]
    score = []
    for b in range(bricks):
        s = rims + b
        for j in reversed(range(rims)):
            s = jnp.where(slots[j] == b, j, s)
        score.append(s)
    place = [
        sum(jnp.where(score[o] < score[b], 1, 0) for o in range(bricks) if o != b)
        for b in range(bricks)
    ]
    held = [
        sum(jnp.where(place[b] == p, b, 0) for b in range(bricks)) for p in range(bricks)
    ]
    for b in range(bricks):
        inv[b] = place[b]
        perm[b] = held[b]
    spot = [sum(jnp.where(slots[j] == b, place[b], 0) for b in range(bricks)) for j in range(rims)]

    def mask_of(b):
        return jnp.where(b < live[0], 1.0, 0.0).astype(jnp.float32)

    low = lax.broadcasted_iota(jnp.int32, (SIDE, pair), 1) < ch
    low1 = lax.broadcasted_iota(jnp.int32, (1, pair), 1) < ch
    loww = lax.broadcasted_iota(jnp.int32, wbuf.shape[2:], 1) < ch

    def take_faces(src, k, p):
        tabx[k][p, 0] = src[p, 0]
        tabx[k][p, 1] = src[p, SIDE - 1]
        for s, y in ((0, 0), (1, SIDE - 1)):
            for x in range(1, SIDE - 1):
                taby[k][p, s, x:x + 1, :] = src[p, x, y:y + 1, :]
        for x in range(1, SIDE - 1):
            at = (x - 1) * pair
            tabz[k][p, :, at:at + pair] = jnp.where(
                low, src[p, x, :, 0:pair], src[p, x, :, width - pair:width]
            )

    def offer(k, j):
        if j > 0:
            for off, tab in ((offx, tabx[k]), (offy, taby[k]), (offz, tabz[k])):
                value = tab[0]
                for p in range(1, j + 1):
                    value = jnp.where(spot[j] == p, tab[p], value)
                off[k, j - 1] = value
        send(k, j)

    def build_weights(k):
        weight_copy(k).wait()
        w = k % 2

        def one(t, carry):
            a = t // 3
            base = pl.multiple_of((t - 3 * a) * ktile, ktile)
            taps = [wbuf[k, 3 * t + i] for i in range(3)]
            turned = [pltpu.roll(tap, ch, 1) for tap in taps]
            none = jnp.zeros(taps[0].shape, jnp.float32)
            rows = taps[0].shape[0]
            for j in range(4):
                first, first_turned = (taps[j], turned[j]) if j < 3 else (none, none)
                second, second_turned = (taps[j - 1], turned[j - 1]) if j > 0 else (none, none)
                blk[j, pl.ds(0, rows, stride=2), :] = jnp.where(loww, first, second_turned)
                blk[j, pl.ds(1, rows, stride=2), :] = jnp.where(loww, first_turned, second)
            for j in range(4):
                block = blk[j]
                hi = block.astype(jnp.bfloat16)
                lo = (block - hi.astype(jnp.float32)).astype(jnp.bfloat16)
                for q in range(2):
                    z = j - 1 + 2 * q
                    row = base + (z if z >= 0 else 5) * ch
                    row = pl.multiple_of(row, ch)
                    lanes = slice(q * pair, (q + 1) * pair)
                    whi[w, a, pl.ds(row, ch), lanes] = hi
                    whi[w, a, pl.ds(pl.multiple_of(row + kdy, ch), ch), lanes] = hi
                    wlo[w, a, pl.ds(row, ch), lanes] = lo
            return carry

        lax.fori_loop(0, 9, one, 0)

    def row_of(center, below, above, mask):
        return jnp.concatenate(
            [
                center[:, :half],
                jnp.where(mask, center[:, half:half + pair], below),
                center[:, half:],
                jnp.where(mask, above, center[:, half - pair:half]),
            ],
            axis=1,
        )

    def build_columns(src, k, p, c):
        tx, ty, tz = tabx[k], taby[k], tabz[k]

        def entry(dx, dy, dz):
            return nb[p, direction_number(dx, dy, dz)]

        def x_row(dx, dy, s, y):
            return row_of(
                tx[entry(dx, dy, 0), s, y:y + 1, :],
                tx[entry(dx, dy, -1), s, y:y + 1, width - pair:width],
                tx[entry(dx, dy, 1), s, y:y + 1, 0:pair],
                low1,
            )

        for dx, xrow, s in ((-1, 0, 1), (1, SIDE + 1, 0)):
            pad[xrow, 1:SIDE + 1, :] = row_of(
                tx[entry(dx, 0, 0), s],
                tx[entry(dx, 0, -1), s, :, width - pair:width],
                tx[entry(dx, 0, 1), s, :, 0:pair],
                low,
            )
            for dy, yrow, y in ((-1, 0, SIDE - 1), (1, SIDE + 1, 0)):
                pad[xrow, yrow:yrow + 1, :] = x_row(dx, dy, s, y)
        nlow, nhigh = entry(0, 0, -1), entry(0, 0, 1)
        for x in range(SIDE):
            if x in (0, SIDE - 1):
                s = 0 if x == 0 else 1
                below = tx[nlow, s, :, width - pair:width]
                above = tx[nhigh, s, :, 0:pair]
            else:
                at = (x - 1) * pair
                below = tz[nlow, :, at:at + pair]
                above = tz[nhigh, :, at:at + pair]
            pad[1 + x, 1:SIDE + 1, :] = row_of(src[p, x], below, above, low)
            if 0 < x < SIDE - 1:
                for s, y in ((0, 0), (1, SIDE - 1)):
                    row = slice(1 + y, 2 + y)
                    pad[1 + x, row, half:half + pair] = jnp.where(
                        low1, src[p, x, y:y + 1, half:half + pair],
                        ty[nlow, s, x:x + 1, width - pair:width],
                    )
                    pad[1 + x, row, width + pair:width + 2 * pair] = jnp.where(
                        low1, ty[nhigh, s, x:x + 1, 0:pair],
                        src[p, x, y:y + 1, half - pair:half],
                    )
        for dy, yrow, s, y in ((-1, 0, 1, SIDE - 1), (1, SIDE + 1, 0, 0)):
            rows = row_of(
                ty[entry(0, dy, 0), s],
                ty[entry(0, dy, -1), s, :, width - pair:width],
                ty[entry(0, dy, 1), s, :, 0:pair],
                low,
            )
            for x in range(1, SIDE - 1):
                pad[1 + x, yrow:yrow + 1, :] = rows[x:x + 1]
            pad[1, yrow:yrow + 1, :] = x_row(0, dy, 0, y)
            pad[SIDE, yrow:yrow + 1, :] = x_row(0, dy, 1, y)
        for x in range(SIDE + 2):
            for dy in range(3):
                v = pad[x, dy:dy + SIDE, :]
                v = jnp.concatenate([v[:, :ktile], v[:, ktile:]], axis=0)
                hi = v.astype(jnp.bfloat16)
                lo = (v - hi.astype(jnp.float32)).astype(jnp.bfloat16)
                cols[c, x, :, dy * ktile:(dy + 1) * ktile] = hi
                cols[c, x, :, kdy + dy * ktile:kdy + (dy + 1) * ktile] = lo

    def convolve(k, c):
        w = k % 2
        rows = SIDE * 2 * SIDE
        left = [cols[c, a:a + SIDE].reshape(rows, 2 * kdy) for a in range(3)]

        def dot(x, y):
            return jnp.dot(x, y, preferred_element_type=jnp.float32)

        tile = 2 * pair
        tiles = -(-2 * kdy // tile) + -(-kdy // tile)
        cut = (tiles // 2) * tile
        one = dot(left[0], whi[w, 0]) + dot(left[0][:, :kdy], wlo[w, 0])
        one = one + dot(left[1][:, :cut], whi[w, 1, :cut])
        two = dot(left[2], whi[w, 2]) + dot(left[2][:, :kdy], wlo[w, 2])
        two = two + dot(left[1][:, cut:], whi[w, 1, cut:]) + dot(left[1][:, :kdy], wlo[w, 1])
        acc[odd] = one
        acc[1 - odd] = two

    def epilogue(k, res, dst, p, at, m):
        bvec = bias[k:k + 1, :]
        bvec = jnp.concatenate([bvec, bvec, bvec, bvec], axis=1)
        for x in range(SIDE):
            for t in range(2):
                row = (2 * x + t) * SIDE
                v = acc[0, row:row + SIDE, :] + acc[1, row:row + SIDE, :] + bvec
                lanes = slice(t * half, (t + 1) * half)
                if res is not None:
                    v = v + res[p, x, :, lanes]
                dst[at, x, :, lanes] = jnp.maximum(v, 0.0) * m

    def mask_features(p, carry):
        cur[p] = feat[perm[p]] * mask_of(perm[p])
        return carry

    feature_copy.wait()
    lax.fori_loop(0, bricks, mask_features, 0)
    for p in range(rims):
        take_faces(cur, 0, p)
    arrivals = sum(jnp.where(has, 1, 0) for has, _ in greeted)
    pl.semaphore_wait(barrier, arrivals)
    for j in range(rims):
        offer(0, j)

    for p in range(rims, bricks):
        take_faces(cur, 0, p)
    for k in range(convs):
        for tab in (tabx[k], taby[k], tabz[k]):
            tab[last] = jnp.zeros(tab.shape[1:], jnp.float32)
    for e in range(last + 1):
        if e < bricks:
            emap[e] = place[e]
        elif e < bricks + rims:
            emap[e] = jnp.where(sp > 0, e, last)
        elif e < bricks + 2 * rims:
            emap[e] = jnp.where(sp < nsp - 1, e, last)
        elif e < bricks + 3 * rims:
            emap[e] = jnp.where(sl > 0, e, last)
        elif e < last:
            emap[e] = jnp.where(sl < nsl - 1, e, last)
        else:
            emap[e] = last

    def remap(j, carry):
        for p in range(bricks):
            nb[p, j] = emap[nbr[perm[p], j]]
        return carry

    lax.fori_loop(0, nbr.shape[1], remap, 0)
    whi[...] = jnp.zeros_like(whi)
    wlo[...] = jnp.zeros_like(wlo)
    build_weights(0)
    bias_copy.wait()
    pass_on(0, range(relayed[0]))

    for k in range(convs):
        src = cur if k % 2 == 0 else hid
        res = None if k % 2 == 0 else cur
        receive(k)
        end = k == convs - 1
        if end:
            dst = stage
            spots = [inv[b] for b in range(bricks)]
        else:
            dst = hid if k % 2 == 0 else cur
            spots = list(range(bricks))
        waiting = [] if end else list(range(relayed[k + 1]))
        build_columns(src, k, spots[0], 0)
        for i in range(bricks):
            p = spots[i]
            if i + 1 < bricks and (end or i != 0):
                build_columns(src, k, spots[i + 1], (i + 1) % 2)
            convolve(k, i % 2)
            if end:
                epilogue(k, res, dst, p, i, mask_of(i))
                out_copy(i).start()
                continue
            epilogue(k, res, dst, p, i, mask_of(perm[i]))
            take_faces(dst, k + 1, i)
            if i < rims:
                offer(k + 1, i)
                if i == 0 and bricks > 1:
                    build_columns(src, k, spots[1], 1)
        if not end:
            pass_on(k + 1, waiting)
            build_weights(k + 1)
    for b in range(bricks):
        out_copy(b).wait()
    for k in range(convs):
        finish_sends(k)


def shards(nsp, nsl, features, live, rim_slots, neighbours, weights, biases):
    bricks, _, _, width = features.shape
    ch = biases.shape[-1]
    convs, taps, _ = weights.shape
    rims = rim_slots.shape[-1]
    entries = bricks + 4 * rims + 1
    pair = 2 * ch
    rows = ch * ch // pair
    planes = weights.reshape(convs, taps, rows, pair).transpose(1, 2, 0, 3)
    half = width // 2
    kdy = 3 * (half + pair)
    inner = (SIDE - 2) * pair
    f32, bf16 = jnp.float32, jnp.bfloat16
    hbm = pl.BlockSpec(memory_space=pltpu.HBM)
    def far(a):
        return pltpu.with_memory_space_constraint(a, pltpu.HBM)

    return pl.pallas_call(
        functools.partial(layers_kernel, nsp, nsl),
        out_shape=jax.ShapeDtypeStruct(features.shape, f32),
        in_specs=[hbm] * 6,
        out_specs=pl.BlockSpec(memory_space=pl.ANY),
        scratch_shapes=[
            pltpu.VMEM(features.shape, f32),
            pltpu.VMEM(biases.shape, f32),
            pltpu.VMEM(features.shape, f32),
            pltpu.VMEM(features.shape, f32),
            pltpu.VMEM(features.shape, f32),
            pltpu.VMEM((convs, max(rims - 1, 1), 2, SIDE, width), f32),
            pltpu.VMEM((convs, max(rims - 1, 1), 2, SIDE, width), f32),
            pltpu.VMEM((convs, max(rims - 1, 1), SIDE, inner), f32),
            pltpu.VMEM((SIDE + 2, 2 * SIDE, width + 2 * pair), f32),
            pltpu.VMEM((2, SIDE + 2, 2 * SIDE, 2 * kdy), bf16),
            pltpu.VMEM((2, 3, 2 * kdy, half), bf16),
            pltpu.VMEM((2, 3, kdy, half), bf16),
            pltpu.VMEM((convs, taps, rows, pair), f32),
            pltpu.VMEM((4, ch, pair), f32),
            pltpu.VMEM((2, SIDE * 2 * SIDE, half), f32),
            pltpu.SMEM(neighbours.shape, jnp.int32),
            pltpu.SMEM(live.shape, jnp.int32),
            pltpu.SMEM(rim_slots.shape, jnp.int32),
            pltpu.SMEM((entries,), jnp.int32),
            pltpu.SMEM((bricks,), jnp.int32),
            pltpu.SMEM((bricks,), jnp.int32),
            pltpu.SMEM(neighbours.shape, jnp.int32),
            pltpu.SemaphoreType.DMA((5,)),
            pltpu.SemaphoreType.DMA((bricks,)),
            pltpu.SemaphoreType.DMA((convs,)),
            pltpu.SemaphoreType.DMA((convs, 4, 3 * rims)),
            pltpu.SemaphoreType.DMA((convs, 4, 3 * rims)),
        ]
        + [pltpu.VMEM((entries, 2, SIDE, width), f32) for _ in range(2 * convs)]
        + [pltpu.VMEM((entries, SIDE, inner), f32) for _ in range(convs)],
        compiler_params=pltpu.CompilerParams(
            collective_id=0, has_side_effects=True, vmem_limit_bytes=26 * 1024 * 1024
        ),
        name="layers",
    )(far(neighbours), live, far(rim_slots), far(features), far(biases), far(planes))


def solution(mesh):
    in_specs = (
        P(("space", "slab"), None, None, None),
        P(("space", "slab")),
        P(("space", "slab"), None),
        P(("space", "slab"), None),
        P(),
        P(),
    )
    out_specs = P(("space", "slab"), None, None, None)
    body = functools.partial(shards, mesh.shape["space"], mesh.shape["slab"])
    return jax.shard_map(body, mesh=mesh, in_specs=in_specs, out_specs=out_specs, check_vma=False)
```
